256 devices in a mesh: dp: 32 (over y, x, core), mp: 8 (over z).
Axes of the slice: x: 4, y: 4, z: 8, core: 2. Of those that a mesh axis runs over, the one named last changes fastest.
Arguments:
- tokens: bfloat16 [2, 4096, 4096], P(None, 'dp', 'mp'), may hold values from -6 to 6
- targets: bfloat16 [2, 4096, 4096], P(None, 'dp', 'mp'), may hold values from -6 to 6
- weight: bfloat16 [4096, 4096], P('mp'), may hold values from -0.09375 to 0.09375
- basis: bfloat16 [4096, 512], replicated, may hold values from -0.09375 to 0.09375
- moment1: float32 [8, 512, 512], P('mp', 'dp'), may hold values from -0.06 to 0.06
- moment2: float32 [8, 512, 512], P('mp', 'dp'), may hold values from 1e-05 to 0.001
Outputs:
- new_weight: bfloat16 [4096, 4096], P('mp')
- new_moment1: float32 [8, 512, 512], P('mp', 'dp')
- new_moment2: float32 [8, 512, 512], P('mp', 'dp')
The draws below stay inside these ranges and needn't reach their ends.
All inputs are finite; a program needn't handle non-finite values.
Results may differ from the reference program's by a relative error of at most 0.009.
Values may be sent and summed in bfloat16 or wider, within the bound.
No kernel may reach another device: no remote copies, remote signals or barrier semaphores. Data moves between devices by JAX's collectives and lax.ppermute only.
A program may use at most 64 MiB of HBM per device.

```python
import math
import jax
import jax.numpy as jnp
from jax import lax

D_OUT = 4096
D_IN = 4096
RANK = 512
TOKENS = 4096
ROWS_MP = 512
N_MP = 8


def block_scale(key, extent, shards, least, top_value):
    def one(axis_at, parts):
        heights = jax.random.uniform(jax.random.fold_in(jax.random.fold_in(key, 6), axis_at), (parts,), jnp.float32, least / len(shards), top_value / len(shards))
        return jnp.repeat(jnp.exp(heights), extent[axis_at] // parts).reshape((-1,) + (1,) * (len(extent) - axis_at - 1))

    loudness = one(*shards[0])
    for cut in shards[1:]:
        loudness = loudness * one(*cut)
    return loudness


def scatter_about(key, dims, deviation, bound, pieces=(), held_as=jnp.bfloat16):
    result = jax.random.normal(key, dims, jnp.float32) * deviation
    if len(pieces) > 0:
        result = block_scale(key, dims, pieces, -0.22, 0.18) * result
    return jnp.clip(result, min=-bound, max=bound).astype(held_as)


def setup_inputs(seed: int = 0) -> dict:
    arg_keys = jax.random.split(jax.random.key(seed), 7)
    return {
        "tokens": scatter_about(arg_keys[0], (2, TOKENS, D_IN), 1.0, 6.0, ((1, 32), (2, 8))),
        "targets": scatter_about(arg_keys[1], (2, TOKENS, D_OUT), 1.0, 6.0, ((1, 32), (2, 8))),
        "weight": scatter_about(arg_keys[2], (D_OUT, D_IN), D_IN ** -0.5, 0.09375, ((0, 8),)),
        "basis": scatter_about(arg_keys[3], (D_IN, RANK), D_IN ** -0.5, 0.09375),
        "moment1": scatter_about(arg_keys[4], (N_MP, ROWS_MP, RANK), 0.01, 0.06, ((0, 8), (1, 32)), jnp.float32),
        "moment2": jnp.clip(jnp.exp(math.log(0.001) - 4.6051703 * jax.random.uniform(arg_keys[5], (N_MP, ROWS_MP, RANK), jnp.float32) ** block_scale(arg_keys[5], (N_MP, ROWS_MP, RANK), ((0, 8), (1, 32)), -0.2, 0.2)), 9.999999747378752e-06, 0.001),
    }


def reference(tokens, targets, weight, basis, moment1, moment2):
    first = moment1.reshape(D_OUT, RANK)
    second = moment2.reshape(D_OUT, RANK)
    current = weight
    for turn in range(2):
        inputs = tokens[turn]
        outputs = jnp.dot(inputs, current.T, preferred_element_type=jnp.float32).astype(jnp.bfloat16)
        errors = (outputs.astype(jnp.float32) - targets[turn].astype(jnp.float32)).astype(jnp.bfloat16)
        reduced = jnp.dot(inputs, basis, preferred_element_type=jnp.float32)
        projected = jnp.dot(errors.astype(jnp.float32).T, reduced, precision=lax.Precision.HIGHEST) / TOKENS
        first = 0.9 * first + 0.1 * projected
        second = 0.95 * second + 0.05 * projected * projected
        direction = (first / (jnp.sqrt(second) + 1e-08)).astype(jnp.bfloat16)
        lifted = jnp.dot(direction, basis.T, preferred_element_type=jnp.float32)
        current = (current.astype(jnp.float32) - 0.02 * lifted).astype(jnp.bfloat16)
    return (current, first.reshape(N_MP, ROWS_MP, RANK), second.reshape(N_MP, ROWS_MP, RANK))
```

```python
import jax
import jax.numpy as jnp
from jax import lax
from jax.sharding import PartitionSpec as P

RATE = 0.02
F32 = jnp.float32
BF16 = jnp.bfloat16


def dot(a, b, dims, precision=None):
    return lax.dot_general(a, b, (dims, ((), ())), precision=precision, preferred_element_type=F32)


def grid_of(mesh_shape):
    chips = mesh_shape // 2
    side = int(round(chips**0.5))
    return side, chips // side


class Plane:
    def __init__(self, n_dp):
        self.n = n_dp
        self.ny, self.nx = grid_of(n_dp)
        i = lax.axis_index("dp")
        self.core = i % 2
        self.x = (i // 2) % self.nx
        self.y = i // (2 * self.nx)

    def shift(self, a, dy, dx, dcore):
        pairs = []
        for i in range(self.n):
            c, x, y = i % 2, (i // 2) % self.nx, i // (2 * self.nx)
            to = (((y + dy) % self.ny) * self.nx + (x + dx) % self.nx) * 2 + (c + dcore) % 2
            pairs.append((i, to))
        return lax.ppermute(a, "dp", pairs)

    def along(self, axis, k):
        return {"y": (k, 0, 0), "x": (0, k, 0), "core": (0, 0, k)}[axis]

    def size(self, axis):
        return {"y": self.ny, "x": self.nx, "core": 2}[axis]

    def at(self, axis):
        return {"y": self.y, "x": self.x, "core": self.core}[axis]

    def reduce_stage(self, a, dim, axis):
        n, at = self.size(axis), self.at(axis)

        def part(k):
            return lax.dynamic_index_in_dim(a, (at + k) % n, dim, keepdims=False)

        arrived = [self.shift(part(k), *self.along(axis, k)) for k in range(1, n)]
        total = part(0).astype(F32)
        for piece in arrived:
            total = total + piece.astype(F32)
        return total

    def gather_stage(self, a, axis):
        n, at = self.size(axis), self.at(axis)
        pieces = [a] + [self.shift(a, *self.along(axis, k)) for k in range(1, n)]
        whole = jnp.zeros((n, *a.shape), a.dtype)
        for k, piece in enumerate(pieces):
            whole = lax.dynamic_update_index_in_dim(whole, piece, (at - k) % n, 0)
        return whole

    def sum_rows(self, a):
        rows = a.shape[0] // self.n
        a = a.reshape(self.ny, self.nx, 2, rows, a.shape[1])
        a = self.reduce_stage(a, 2, "core").astype(BF16)
        a = self.reduce_stage(a, 1, "x").astype(BF16)
        return self.reduce_stage(a, 0, "y")

    def gather_rows(self, a):
        rows, cols = a.shape
        a = self.gather_stage(a, "x")
        a = self.gather_stage(a, "y")
        a = self.gather_stage(a, "core")
        return a.transpose(1, 2, 0, 3, 4).reshape(self.n * rows, cols)


def local(tokens, targets, weight, basis, moment1, moment2):
    n_mp = lax.axis_size("mp")
    n_dp = lax.axis_size("dp")
    j = lax.axis_index("mp")
    plane = Plane(n_dp)
    steps, toks, width = tokens.shape
    total_tokens = toks * n_dp
    rank = basis.shape[1]
    rows_mp = weight.shape[0]

    def ahead(a, k):
        return lax.ppermute(a, "mp", [(i, (i + k) % n_mp) for i in range(n_mp)])

    own_basis = lax.dynamic_slice(basis, (j * width, 0), (width, rank))
    parts = dot(tokens[1], own_basis, ((1,), (0,))).astype(BF16)
    parts = parts.reshape(n_mp, toks // n_mp, rank)
    few = lax.dynamic_index_in_dim(parts, j, 0, keepdims=False).astype(F32)
    for k in range(1, n_mp):
        few = few + ahead(lax.dynamic_index_in_dim(parts, (j + k) % n_mp, 0, keepdims=False), k).astype(F32)
    few = few.astype(BF16)
    gram = plane.sum_rows(dot(few, few, ((0,), (0,))).astype(BF16)).astype(BF16)
    gram_rows = gram.astype(F32)
    for k in range(1, n_mp):
        gram_rows = gram_rows + ahead(gram, k).astype(F32)
    gram = plane.gather_rows(gram_rows.astype(BF16))

    right, left = tokens, tokens
    outputs = jnp.zeros((steps * toks, rows_mp), F32)
    reduced = jnp.zeros((steps * toks, rank), F32)

    def add(outputs, reduced, chunk, k):
        at = ((j - k) % n_mp) * width
        chunk = chunk.reshape(steps * toks, width)
        w = lax.dynamic_slice(weight, (0, at), (rows_mp, width))
        b = lax.dynamic_slice(basis, (at, 0), (width, rank))
        return outputs + dot(chunk, w, ((1,), (1,))), reduced + dot(chunk, b, ((1,), (0,)))

    outputs, reduced = add(outputs, reduced, tokens, 0)
    half = n_mp // 2
    for k in range(1, half):
        right, left = ahead(right, 1), ahead(left, -1)
        outputs, reduced = add(outputs, reduced, right, k)
        outputs, reduced = add(outputs, reduced, left, -k)
    last = jnp.stack([ahead(right[0], 1), ahead(left[1], -1)])
    outputs, reduced = add(outputs, reduced, last, half)

    errors = outputs.astype(BF16).astype(F32) - targets.reshape(steps * toks, rows_mp).astype(F32)
    errors = errors.astype(BF16).astype(F32).reshape(steps, toks, rows_mp)
    reduced = reduced.reshape(steps, toks, rank)
    rows = rows_mp // n_dp
    sums = [
        dot(errors[s], reduced[s], ((0,), (0,)), lax.Precision.HIGHEST).astype(BF16).reshape(n_dp, rows, rank)
        for s in range(steps)
    ]
    sums = plane.sum_rows(jnp.concatenate(sums, axis=1).reshape(n_dp * steps * rows, rank))
    sums = sums.reshape(steps, rows, rank)

    def update(first, second, projected):
        first = 0.9 * first + 0.1 * projected
        second = 0.95 * second + 0.05 * projected * projected
        direction = (first / (jnp.sqrt(second) + 1e-08)).astype(BF16)
        return first, second, direction

    first, second, d0 = update(moment1[0], moment2[0], sums[0] / total_tokens)
    moved = dot(d0, gram, ((1,), (0,)))
    first, second, d1 = update(first, second, (sums[1] - RATE * moved) / total_tokens)
    both = (d0.astype(F32) + d1.astype(F32)).astype(BF16)
    lifted = dot(plane.gather_rows(both), basis, ((1,), (1,)))
    new_weight = (weight.astype(F32) - RATE * lifted).astype(BF16)
    return (new_weight, first[None], second[None])


def solution(mesh):
    in_specs = (
        P(None, "dp", "mp"),
        P(None, "dp", "mp"),
        P("mp", None),
        P(),
        P("mp", "dp", None),
        P("mp", "dp", None),
    )
    out_specs = (P("mp", None), P("mp", "dp", None), P("mp", "dp", None))
    return jax.shard_map(local, mesh=mesh, in_specs=in_specs, out_specs=out_specs, check_vma=False)
```

```python
import jax
import jax.numpy as jnp
from jax import lax
from jax.sharding import PartitionSpec as P

RATE = 0.02
F32 = jnp.float32
BF16 = jnp.bfloat16


def dot(a, b, dims, precision=None):
    return lax.dot_general(a, b, (dims, ((), ())), precision=precision, preferred_element_type=F32)


class Plane:
    def __init__(self, n_dp):
        self.chips = n_dp // 2
        self.core = lax.axis_index("dp") % 2
        self.swap = [(i, i ^ 1) for i in range(n_dp)]
        self.groups = [[2 * chip + core for chip in range(self.chips)] for core in range(2)]

    def other_core(self, a):
        return lax.ppermute(a, "dp", self.swap)

    def chips_exchange(self, a):
        return lax.all_to_all(a, "dp", split_axis=0, concat_axis=0, tiled=True, axis_index_groups=self.groups)

    def sum_rows(self, a):
        away = self.other_core(lax.dynamic_index_in_dim(a, 1 - self.core, 1, keepdims=False))
        kept = lax.dynamic_index_in_dim(a, self.core, 1, keepdims=False)
        chip = (kept.astype(F32) + away.astype(F32)).astype(BF16)
        return self.chips_exchange(chip).astype(F32).sum(axis=0)

    def gather_rows(self, a):
        mine = self.chips_exchange(jnp.broadcast_to(a, (self.chips, *a.shape)))
        other = self.other_core(mine)
        first = jnp.where(self.core == 0, mine, other)
        second = jnp.where(self.core == 0, other, mine)
        return jnp.stack([first, second], axis=1).reshape(2 * self.chips * a.shape[0], a.shape[1])


def local(tokens, targets, weight, basis, moment1, moment2):
    n_mp = lax.axis_size("mp")
    n_dp = lax.axis_size("dp")
    j = lax.axis_index("mp")
    plane = Plane(n_dp)
    steps, toks, width = tokens.shape
    total_tokens = toks * n_dp
    rank = basis.shape[1]
    rows_mp = weight.shape[0]

    def ahead(a, k):
        return lax.ppermute(a, "mp", [(i, (i + k) % n_mp) for i in range(n_mp)])

    right, left = tokens, tokens
    outputs = jnp.zeros((steps * toks, rows_mp), F32)
    reduced = jnp.zeros((steps * toks, rank), F32)

    def add(outputs, reduced, chunk, k):
        at = ((j - k) % n_mp) * width
        chunk = chunk.reshape(steps * toks, width)
        w = lax.dynamic_slice(weight, (0, at), (rows_mp, width))
        b = lax.dynamic_slice(basis, (at, 0), (width, rank))
        return outputs + dot(chunk, w, ((1,), (1,))), reduced + dot(chunk, b, ((1,), (0,)))

    outputs, reduced = add(outputs, reduced, tokens, 0)
    half = n_mp // 2
    for k in range(1, half):
        right, left = ahead(right, 1), ahead(left, -1)
        outputs, reduced = add(outputs, reduced, right, k)
        outputs, reduced = add(outputs, reduced, left, -k)
    last = jnp.stack([ahead(right[0], 1), ahead(left[1], -1)])
    outputs, reduced = add(outputs, reduced, last, half)

    errors = outputs.astype(BF16).astype(F32) - targets.reshape(steps * toks, rows_mp).astype(F32)
    errors = errors.astype(BF16).reshape(steps, toks, rows_mp)
    reduced = reduced.astype(BF16).reshape(steps, toks, rank)
    rows = rows_mp // n_dp
    lefts = [errors[0], errors[1], reduced[1]]
    rights = [reduced[0], reduced[1], reduced[1]]
    parts = [
        dot(l, r, ((0,), (0,))).astype(BF16).reshape(n_dp // 2, 2, -1, rank) for l, r in zip(lefts, rights)
    ]
    sums = plane.sum_rows(jnp.concatenate(parts, axis=2))
    gram = plane.gather_rows(sums[2 * rows :].astype(BF16))
    sums = sums[: 2 * rows].reshape(steps, rows, rank)

    def update(first, second, projected):
        first = 0.9 * first + 0.1 * projected
        second = 0.95 * second + 0.05 * projected * projected
        direction = (first / (jnp.sqrt(second) + 1e-08)).astype(BF16)
        return first, second, direction

    first, second, d0 = update(moment1[0], moment2[0], sums[0] / total_tokens)
    moved = dot(d0, gram, ((1,), (0,)))
    first, second, d1 = update(first, second, (sums[1] - RATE * moved) / total_tokens)
    both = (d0.astype(F32) + d1.astype(F32)).astype(BF16)
    lifted = dot(plane.gather_rows(both), basis, ((1,), (1,)))
    new_weight = (weight.astype(F32) - RATE * lifted).astype(BF16)
    return (new_weight, first[None], second[None])


def solution(mesh):
    in_specs = (
        P(None, "dp", "mp"),
        P(None, "dp", "mp"),
        P("mp", None),
        P(),
        P("mp", "dp", None),
        P("mp", "dp", None),
    )
    out_specs = (P("mp", None), P("mp", "dp", None), P("mp", "dp", None))
    return jax.shard_map(local, mesh=mesh, in_specs=in_specs, out_specs=out_specs, check_vma=False)
```

```python
import jax
import jax.numpy as jnp
from jax import lax
from jax.sharding import PartitionSpec as P

RATE = 0.02
F32 = jnp.float32
BF16 = jnp.bfloat16


def dot(a, b, dims):
    return lax.dot_general(a, b, (dims, ((), ())), preferred_element_type=F32)


def body(tokens, targets, weight, basis, moment1, moment2):
    n_mp = lax.axis_size("mp")
    n_dp = lax.axis_size("dp")
    j = lax.axis_index("mp")
    core = lax.axis_index("dp") % 2
    chips = n_dp // 2
    steps, toks, width = tokens.shape
    total_tokens = toks * n_dp
    rank = basis.shape[1]
    rows_mp = weight.shape[0]
    rows = rows_mp // n_dp
    groups = [[2 * chip + c for chip in range(chips)] for c in range(2)]

    def ahead(a, k):
        return lax.ppermute(a, "mp", [(i, (i + k) % n_mp) for i in range(n_mp)])

    def other_core(a):
        return lax.ppermute(a, "dp", [(i, i ^ 1) for i in range(n_dp)])

    def exchange(a):
        return lax.all_to_all(a, "dp", split_axis=0, concat_axis=0, tiled=True, axis_index_groups=groups)

    def gather_rows(a):
        mine = exchange(jnp.broadcast_to(a, (chips, *a.shape)))
        other = other_core(mine)
        both = [jnp.where(core == 0, mine, other), jnp.where(core == 0, other, mine)]
        return jnp.stack(both, axis=1).reshape(n_dp * a.shape[0], a.shape[1])

    features = jnp.zeros((steps * toks, n_mp * width), BF16)

    def put(features, chunk, s, k):
        return lax.dynamic_update_slice(features, chunk, (s * toks, ((j - k) % n_mp) * width))

    half = n_mp // 2
    right = lax.optimization_barrier([tokens[s] for s in range(steps)])
    left = list(right)
    for s in range(steps):
        features = put(features, right[s], s, 0)
    for k in range(1, half):
        for s in (1, 0):
            right[s] = ahead(right[s], 1)
            left[s] = ahead(left[s], -1)
            features = put(features, right[s], s, k)
            features = put(features, left[s], s, -k)
    right[1] = ahead(right[1], 1)
    left[0] = ahead(left[0], -1)
    features = put(features, right[1], 1, half)
    features = put(features, left[0], 0, half)
    outputs, reduced = lax.optimization_barrier(
        (dot(features, weight, ((1,), (1,))), dot(features, basis, ((1,), (0,))).astype(BF16))
    )

    reduced = reduced.reshape(steps, toks, rank)
    errors = outputs.astype(BF16).astype(F32) - targets.reshape(steps * toks, rows_mp).astype(F32)
    errors = errors.astype(BF16).reshape(steps, toks, rows_mp)
    pairs = [(errors[0], reduced[0]), (errors[1], reduced[1]), (reduced[1], reduced[1])]
    parts = [dot(a, b, ((0,), (0,))).astype(BF16).reshape(chips, 2, -1, rank) for a, b in pairs]
    parts = jnp.concatenate(parts, axis=2)
    away = other_core(lax.dynamic_index_in_dim(parts, 1 - core, 1, keepdims=False))
    kept = lax.dynamic_index_in_dim(parts, core, 1, keepdims=False)
    sums = exchange((kept.astype(F32) + away.astype(F32)).astype(BF16)).astype(F32).sum(axis=0)
    gram = gather_rows(sums[2 * rows :].astype(BF16))

    def update(first, second, projected):
        first = 0.9 * first + 0.1 * projected
        second = 0.95 * second + 0.05 * projected * projected
        direction = (first / (jnp.sqrt(second) + 1e-08)).astype(BF16)
        return first, second, direction

    first, second, d0 = update(moment1[0], moment2[0], sums[:rows] / total_tokens)
    moved = dot(d0, gram, ((1,), (0,)))
    first, second, d1 = update(first, second, (sums[rows : 2 * rows] - RATE * moved) / total_tokens)
    both = (d0.astype(F32) + d1.astype(F32)).astype(BF16)
    lifted = dot(gather_rows(both), basis, ((1,), (1,)))
    new_weight = (weight.astype(F32) - RATE * lifted).astype(BF16)
    return (new_weight, first[None], second[None])


def solution(mesh):
    in_specs = (
        P(None, "dp", "mp"),
        P(None, "dp", "mp"),
        P("mp", None),
        P(),
        P("mp", "dp", None),
        P("mp", "dp", None),
    )
    out_specs = (P("mp", None), P("mp", "dp", None), P("mp", "dp", None))
    return jax.shard_map(body, mesh=mesh, in_specs=in_specs, out_specs=out_specs, check_vma=False)
```

```python
import jax
import jax.numpy as jnp
from jax import lax
from jax.sharding import PartitionSpec as P

RATE = 0.02
F32 = jnp.float32
BF16 = jnp.bfloat16


def dot(a, b, dims):
    return lax.dot_general(a, b, (dims, ((), ())), preferred_element_type=F32)


def body(tokens, targets, weight, basis, moment1, moment2):
    n_mp = lax.axis_size("mp")
    n_dp = lax.axis_size("dp")
    j = lax.axis_index("mp")
    core = lax.axis_index("dp") % 2
    chips = n_dp // 2
    steps, toks, width = tokens.shape
    total_tokens = toks * n_dp
    rank = basis.shape[1]
    rows_mp = weight.shape[0]
    rows = rows_mp // n_dp
    groups = [[2 * chip + c for chip in range(chips)] for c in range(2)]

    def ahead(a, k):
        return lax.ppermute(a, "mp", [(i, (i + k) % n_mp) for i in range(n_mp)])

    def other_core(a):
        return lax.ppermute(a, "dp", [(i, i ^ 1) for i in range(n_dp)])

    def exchange(a):
        return lax.all_to_all(a, "dp", split_axis=0, concat_axis=0, tiled=True, axis_index_groups=groups)

    def pair_rows(parts):
        away = other_core(lax.dynamic_index_in_dim(parts, 1 - core, 1, keepdims=False))
        kept = lax.dynamic_index_in_dim(parts, core, 1, keepdims=False)
        return (kept.astype(F32) + away.astype(F32)).astype(BF16)

    def by_owner(a, b):
        return dot(a, b, ((0,), (0,))).astype(BF16).reshape(chips, 2, -1, rank)

    def both_cores(mine):
        other = other_core(mine)
        both = [jnp.where(core == 0, mine, other), jnp.where(core == 0, other, mine)]
        return jnp.stack(both, axis=1).reshape(-1, mine.shape[-1])

    def for_each_chip(a):
        return jnp.broadcast_to(a, (chips, *a.shape))

    half = n_mp // 2
    own = lax.optimization_barrier([tokens[s] for s in range(steps)])
    right, left = list(own), list(own)

    def put(features, chunk, k):
        return lax.dynamic_update_slice(features, chunk, (0, ((j - k) % n_mp) * width))

    features = [put(jnp.zeros((toks, n_mp * width), BF16), own[s], 0) for s in range(steps)]
    for k in range(1, half):
        for s in (1, 0):
            right[s] = ahead(right[s], 1)
            left[s] = ahead(left[s], -1)
            features[s] = put(put(features[s], right[s], k), left[s], -k)
    last1 = ahead(right[1], 1)
    last0 = ahead(left[0], -1)

    features[1] = put(features[1], last1, half)
    reduced1 = lax.optimization_barrier(dot(features[1], basis, ((1,), (0,))).astype(BF16))
    gram_parts = by_owner(reduced1, reduced1)
    gram_parts, last0, features[1] = lax.optimization_barrier((gram_parts, last0, features[1]))
    features[0] = put(features[0], last0, half)
    reduced0 = lax.optimization_barrier(dot(features[0], basis, ((1,), (0,))).astype(BF16))
    pair = pair_rows(gram_parts)
    arrived = exchange(pair)
    gram_rows = arrived.astype(F32).sum(axis=0).astype(BF16)

    reduced = [reduced0, reduced1]
    outputs = [dot(features[s], weight, ((1,), (1,))) for s in range(steps)]
    outputs = lax.optimization_barrier(outputs)
    errors = [(outputs[s].astype(BF16).astype(F32) - targets[s].astype(F32)).astype(BF16) for s in range(steps)]
    parts = jnp.concatenate([by_owner(errors[s], reduced[s]) for s in range(steps)], axis=2)
    pair = pair_rows(parts)
    arrived = exchange(jnp.concatenate([pair, for_each_chip(gram_rows)], axis=1))
    sums = arrived[:, : steps * rows].astype(F32).sum(axis=0)
    gram = both_cores(arrived[:, steps * rows :])

    def update(first, second, projected):
        first = 0.9 * first + 0.1 * projected
        second = 0.95 * second + 0.05 * projected * projected
        direction = (first / (jnp.sqrt(second) + 1e-08)).astype(BF16)
        return first, second, direction

    first, second, d0 = update(moment1[0], moment2[0], sums[:rows] / total_tokens)
    moved = dot(d0, gram, ((1,), (0,)))
    first, second, d1 = update(first, second, (sums[rows:] - RATE * moved) / total_tokens)
    both = (d0.astype(F32) + d1.astype(F32)).astype(BF16)
    lifted = dot(both_cores(exchange(for_each_chip(both))), basis, ((1,), (1,)))
    new_weight = (weight.astype(F32) - RATE * lifted).astype(BF16)
    return (new_weight, first[None], second[None])


def solution(mesh):
    in_specs = (
        P(None, "dp", "mp"),
        P(None, "dp", "mp"),
        P("mp", None),
        P(),
        P("mp", "dp", None),
        P("mp", "dp", None),
    )
    out_specs = (P("mp", None), P("mp", "dp", None), P("mp", "dp", None))
    return jax.shard_map(body, mesh=mesh, in_specs=in_specs, out_specs=out_specs, check_vma=False)
```
